32 devices in a mesh: mem: 4 (over y, x), ty: 4 (over z), tx: 2 (over core).
Axes of the slice: x: 2, y: 2, z: 4, core: 2. Of those that a mesh axis runs over, the one named last changes fastest.
Arguments:
- controls: float32 [16, 512, 1024], P(('mem', 'ty'), None, 'tx'), may hold values from -6 to 6
- perturbations: bfloat16 [16, 512, 1024], P(None, ('mem', 'ty'), 'tx'), may hold values from -6 to 6
- kx: bfloat16 [512, 1024], P(None, 'tx'), may hold values from 0.11 to 0.24
- ky: bfloat16 [512, 1024], P(None, 'tx'), may hold values from 0.11 to 0.24
- wet: int32 [512, 1024], P(None, 'tx'), may hold values from 0 to 1, as said below
Outputs:
- smoothed: float32 [16, 512, 1024], P(('mem', 'ty'), None, 'tx')
- increment: float32 [2, 512, 1024], P(None, ('mem', 'ty'), 'tx')
The draws below stay inside these ranges and needn't reach their ends.
Inputs may be any that keep to these rules, and one draw needn't show every extreme that they name: `wet`: rows 0 and 511 are land (0) in every column.
All inputs are finite; a program needn't handle non-finite values.
Results may differ from the reference program's by a relative error of at most 0.0003.
Values may be sent and summed in bfloat16 or wider, within the bound.
A program may use at most 64 MiB of HBM per device.

```python
import jax
import jax.numpy as jnp
from jax import lax

MEMBERS = 8
STEPS = 8
SLABS = 16
LEV = 2
NY = 512
NX = 1024


def draw_wet(key, part):
    cell_key, block_key = jax.random.split(key)
    cell_draw = jax.random.randint(cell_key, (NY, NX), 0, 100) < 98
    blocks = jax.random.randint(block_key, (NY // 4, NX // 4), 0, 100) < 99
    blocks = jnp.repeat(jnp.repeat(blocks, 4, axis=0), 4, axis=1)
    row_index = jnp.arange(NY)[:, None]
    interior = (row_index > 0) & (row_index < NY - 1)
    return (cell_draw & blocks & interior).astype(jnp.int32)


def coefficient_field(key, salt):
    uniform_draw = jax.random.uniform(jax.random.fold_in(key, salt), (NY, NX), jnp.float32)
    factor = 1.0 - 0.5 * uniform_draw * uniform_draw
    return (0.23925781 * factor).astype(jnp.bfloat16)


def draw_kx(key, part):
    return coefficient_field(key, 1101)


def draw_ky(key, part):
    return coefficient_field(key, 1202)


def draw_controls(key, part):
    noise_key = jax.random.fold_in(key, 1303)
    noise = jax.random.normal(noise_key, (SLABS, NY, NX), jnp.float32)
    row_index = jnp.arange(NY, dtype=jnp.int32)[:, None]
    col_index = jnp.arange(NX, dtype=jnp.int32)[None, :]
    parity = ((row_index + col_index) % 2).astype(jnp.float32)
    checker = 3.0 * (1.0 - 2.0 * parity)
    return jnp.clip(noise + checker[None, :, :], -6.0, 6.0)


def levels(rng, extent, shards, smallest, top_value):
    loudness, own = 1.0, jax.random.fold_in(rng, 6)
    for axis_at, blocks in shards:
        heights = jnp.exp(jax.random.uniform(jax.random.fold_in(own, axis_at), (blocks,), jnp.float32, smallest / len(shards), top_value / len(shards)))
        loudness = loudness * jnp.repeat(heights, extent[axis_at] // blocks).reshape([-1 if axis == axis_at else 1 for axis in range(len(extent))])
    return loudness


def normal_values(key, extent, deviation, limit, shards=(), kind=jnp.bfloat16):
    loudness = levels(key, extent, shards, -0.22, 0.18) if shards else 1.0
    array = jax.random.normal(key, extent, jnp.float32) * deviation * loudness
    return jnp.minimum(jnp.maximum(array, -limit), limit).astype(kind)


def setup_inputs(seed: int = 0) -> dict:
    key_of = jax.random.split(jax.random.key(seed), 6)
    controls = draw_controls(jax.random.fold_in(key_of[5], 71), 0)
    perturbations = normal_values(key_of[1], (SLABS, NY, NX), 1.0, 6.0, ((1, 16), (2, 2)))
    kx = draw_kx(jax.random.fold_in(key_of[5], 71), 0)
    ky = draw_ky(jax.random.fold_in(key_of[5], 71), 0)
    wet = draw_wet(jax.random.fold_in(key_of[5], 71), 0)
    return dict(controls=controls, perturbations=perturbations, kx=kx, ky=ky, wet=wet)


def reference(controls, perturbations, kx, ky, wet):
    ocean = wet.astype(jnp.float32)
    zonal_coef = kx.astype(jnp.float32) * ocean
    merid_coef = ky.astype(jnp.float32) * ocean
    face_east = jnp.minimum(zonal_coef, jnp.roll(zonal_coef, -1, 1))
    face_west = jnp.roll(face_east, 1, 1)
    zero_row = jnp.zeros((1, NX), jnp.float32)
    merid_next = jnp.concatenate([merid_coef[1:], zero_row], 0)
    face_north = jnp.minimum(merid_coef, merid_next)
    face_south = jnp.concatenate([zero_row, face_north[:-1]], 0)
    smoothed = controls
    zero_slab = jnp.zeros((SLABS, 1, NX), jnp.float32)
    for step_index in range(STEPS):
        east_cell = jnp.roll(smoothed, -1, 2)
        west_cell = jnp.roll(smoothed, 1, 2)
        north_cell = jnp.concatenate([smoothed[:, 1:], zero_slab], 1)
        south_cell = jnp.concatenate([zero_slab, smoothed[:, :-1]], 1)
        smoothed = smoothed + (face_east * (east_cell - smoothed) - face_west * (smoothed - west_cell)) + (face_north * (north_cell - smoothed) - face_south * (smoothed - south_cell))
    member_scale = 1.0 / jnp.sqrt(jnp.float32(MEMBERS - 1))
    product = perturbations.astype(jnp.float32).reshape(MEMBERS, LEV, NY, NX) * smoothed.reshape(MEMBERS, LEV, NY, NX)
    increment = lax.optimization_barrier(jnp.sum(product, axis=0)) * member_scale
    return (smoothed, increment)
```

```python
import functools
import math

import jax
import jax.numpy as jnp
from jax import lax
from jax.experimental import pallas as pl
from jax.experimental.pallas import tpu as pltpu
from jax.sharding import PartitionSpec as P

MEMBERS = 8
STEPS = 8
LANES = 128
GROUP = 8
EDGE = 2 * GROUP
MASK = 64
PARTS = 6
CODE = 32767.0
MESH = pl.DeviceIdType.MESH


def kernel(
    mems, tys, txs, ctrl, pert, kx, ky, wet, final, out_i,
    kx_in, ky_in, wet_in, f_in, pert_in, plain, masked, cells, other, fe, fn, south, zonal, up, down,
    send, recv, peak, peaks,
    in_sem, edge_send, edge_recv, tile_send, tile_recv, peak_send, peak_recv,
):
    tiles = mems * tys
    own, rows, _ = kx_in.shape
    cols = own * LANES
    fold = rows // LANES
    tile = rows // tiles
    levels = tiles // MEMBERS
    me_mem, me_ty, me_tx = lax.axis_index("mem"), lax.axis_index("ty"), lax.axis_index("tx")
    me = me_mem * tys + me_ty
    first = me + 1
    right, left = lax.rem(me_tx + 1, txs), lax.rem(me_tx + txs - 1, txs)
    sides = (right,) if txs == 2 else (right, left)

    def strip_loads(n, src, dst):
        return [
            pltpu.make_async_copy(src(pl.ds(c * LANES, LANES)), dst.at[c], in_sem.at[n, c]) for c in range(own)
        ]

    loads = [
        strip_loads(0, lambda s: kx.at[:, s], kx_in),
        strip_loads(1, lambda s: ky.at[:, s], ky_in),
        strip_loads(2, lambda s: wet.at[:, s], wet_in),
        strip_loads(3, lambda s: ctrl.at[0, :, s], f_in),
        strip_loads(4, lambda s: pert.at[:, :, s], pert_in),
    ]
    order = (0, own - 1, *range(1, own - 1))
    for group in (loads[:3], loads[3:4]):
        for c in order:
            for load in group:
                load[c].start()
    for load in loads[4]:
        load.start()

    barrier = pltpu.get_barrier_semaphore()
    for side in sides:
        pl.semaphore_signal(barrier, inc=1, device_id={"tx": side}, device_id_type=MESH)

    @pl.loop(1, tiles)
    def _(step):
        to = lax.rem(me + step, tiles)
        pl.semaphore_signal(
            barrier, inc=1, device_id={"mem": to // tys, "ty": lax.rem(to, tys)}, device_id_type=MESH
        )

    def turn_in(src, dst, c):
        for q in range(fold):
            dst[q, EDGE + c * LANES : EDGE + (c + 1) * LANES, :] = src[pl.ds(q, LANES, stride=fold), :].T

    def mask(c):
        for load in loads[:3]:
            load[c].wait()

        @pl.loop(0, rows // MASK)
        def _(n):
            at = pl.ds(pl.multiple_of(n * MASK, MASK), MASK)
            ocean = wet_in[c, at, :].astype(jnp.float32)
            plain[0, at, :] = kx_in[c, at, :].astype(jnp.float32) * ocean
            plain[1, at, :] = ky_in[c, at, :].astype(jnp.float32) * ocean

        for n in range(2):
            turn_in(plain.at[n], masked.at[n], c)

    def field(c):
        loads[3][c].wait()
        turn_in(f_in.at[c], cells, c)

    for c in order[:2]:
        mask(c)
    for c in order[:2]:
        field(c)

    pl.semaphore_wait(barrier, tiles - 1 + len(sides))
    edges = []
    for n, (side, src, dst) in enumerate(((left, EDGE, EDGE + cols), (right, EDGE + cols - GROUP, EDGE - GROUP))):
        for m, ref in enumerate((masked.at[0], masked.at[1], cells)):
            edges.append(
                pltpu.make_async_remote_copy(
                    src_ref=ref.at[:, pl.ds(src, GROUP), :], dst_ref=ref.at[:, pl.ds(dst, GROUP), :],
                    send_sem=edge_send.at[n, m], recv_sem=edge_recv.at[n, m],
                    device_id={"tx": side}, device_id_type=MESH,
                )
            )
            edges[-1].start()

    for c in order[2:]:
        mask(c)
    for c in order[2:]:
        field(c)

    def coefficients(base, count):
        at, after = pl.ds(base, count), pl.ds(base + 1, count)
        gys = [masked[1, q, at, :] for q in range(fold)]
        for q in range(fold):
            fe[q, at, :] = jnp.minimum(masked[0, q, at, :], masked[0, q, after, :])
            north = gys[q + 1] if q + 1 < fold else pltpu.roll(gys[0], LANES - 1, 1)
            fn[q, at, :] = jnp.minimum(gys[q], north)
        south[at, :] = jnp.minimum(gys[0], pltpu.roll(gys[-1], 1, 1))

    def largest(base, count, most):
        for q in range(fold):
            for g in range(0, count, GROUP):
                most = jnp.maximum(most, jnp.abs(cells[q, pl.ds(base + g, GROUP), :]))
        return most

    block = cols // 4
    for n in range(4):
        coefficients(EDGE + n * block, block if n < 3 else block - GROUP)

    most = lax.fori_loop(
        0, cols // GROUP // 8,
        lambda n, most: largest(pl.multiple_of(EDGE + n * 8 * GROUP, GROUP), 8 * GROUP, most),
        jnp.full((GROUP, LANES), 1e-30, jnp.float32),
    )

    for edge in edges:
        edge.wait()
    coefficients(EDGE - GROUP, GROUP)
    coefficients(EDGE + cols - GROUP, 2 * GROUP)
    most = largest(EDGE - GROUP, GROUP, largest(EDGE + cols, GROUP, most))
    most = jnp.max(jnp.max(most, axis=0, keepdims=True), axis=1, keepdims=True)
    peak[...] = jnp.broadcast_to(most, (GROUP, LANES))

    wide = cols + 2 * GROUP
    lowest = EDGE - GROUP
    span = wide // PARTS

    def advance(old, new):
        whole = pl.ds(lowest, wide)
        up[whole, :] = pltpu.roll(old[0, whole, :], LANES - 1, 1)
        down[whole, :] = pltpu.roll(old[fold - 1, whole, :], 1, 1)

        @pl.loop(0, PARTS)
        def _(n):
            for g in range(0, span, GROUP):
                base = pl.multiple_of(lowest + n * span, GROUP) + g
                at, after, back = pl.ds(base, GROUP), pl.ds(base + 1, GROUP), pl.ds(base - 1, GROUP)
                here = [old[q, at, :] for q in range(fold)]
                flux_s = south[at, :] * (here[0] - down[at, :])
                for q in range(fold):
                    north = here[q + 1] if q + 1 < fold else up[at, :]
                    flux_n = fn[q, at, :] * (north - here[q])
                    flux_e = fe[q, at, :] * (old[q, after, :] - here[q])
                    zonal[q, at, :] = flux_e
                    new[q, at, :] = here[q] + (flux_e - zonal[q, back, :]) + (flux_n - flux_s)
                    flux_s = flux_n

    @pl.loop(0, STEPS // 2)
    def _(_):
        advance(cells, other)
        advance(other, cells)

    for c in range(own):
        for q in range(fold):
            final[c, pl.ds(q, LANES, stride=fold), :] = cells[q, EDGE + c * LANES : EDGE + (c + 1) * LANES, :].T

    def peak_copy(t):
        to = lax.rem(first + t, tiles)
        return pltpu.make_async_remote_copy(
            src_ref=peak, dst_ref=peaks.at[t],
            send_sem=peak_send.at[t], recv_sem=peak_recv.at[t],
            device_id={"mem": to // tys, "ty": lax.rem(to, tys)}, device_id_type=MESH,
        )

    def tile_copy(t):
        to = lax.rem(first + t, tiles)
        return pltpu.make_async_remote_copy(
            src_ref=send.at[t], dst_ref=recv.at[t],
            send_sem=tile_send.at[t], recv_sem=tile_recv.at[t],
            device_id={"mem": to // tys, "ty": lax.rem(to, tys)}, device_id_type=MESH,
        )

    factor = CODE * lax.rsqrt(peak[:1, :1])

    def tile_of(c, which):
        return final[c, pl.ds(pl.multiple_of(which * tile, tile), tile), :]

    @pl.loop(0, tiles - 1)
    def _(t):
        which = lax.rem(first + t, tiles)
        for c in range(own):
            done = tile_of(c, which)
            code = done * lax.rsqrt(jnp.maximum(jnp.abs(done), 1e-37)) * factor
            code = jnp.round(jnp.clip(code, -CODE, CODE))
            send[t, c] = code.astype(jnp.int32).astype(jnp.int16)
        tile_copy(t).start()
        peak_copy(t).start()

    for load in loads[4]:
        load.wait()
    scale = 1.0 / math.sqrt(MEMBERS - 1)
    for level in range(levels):
        out_i[level] = jnp.zeros(out_i.shape[1:], jnp.float32)
    for c in range(own):
        mine = tile_of(c, me) * scale
        out_i[lax.rem(me, levels), :, c * LANES : (c + 1) * LANES] = pert_in[c, me].astype(jnp.float32) * mine

    @pl.loop(0, tiles - 1)
    def _(t):
        tile_copy(t).wait_recv()
        slab = lax.rem(me - 1 - t + 2 * tiles, tiles)
        peak_copy(t).wait_recv()
        unit = peaks[t, :1, :1] * (scale / (CODE * CODE))
        level = lax.rem(slab, levels)
        for c in range(own):
            at = slice(c * LANES, (c + 1) * LANES)
            code = recv[t, c].astype(jnp.float32)
            got = code * jnp.abs(code) * unit
            out_i[level, :, at] = out_i[level, :, at] + pert_in[c, slab].astype(jnp.float32) * got

    @pl.loop(0, tiles - 1)
    def _(t):
        tile_copy(t).wait_send()
        peak_copy(t).wait_send()


def store(final, total, out_s, out_i, sem):
    rows, strips = out_s.shape[1], out_s.shape[2] // LANES
    copies = [
        pltpu.make_async_copy(
            final.at[c], out_s.at[0, :, pl.ds(c * LANES, LANES)], sem.at[c]
        )
        for c in range(strips)
    ]
    copies.append(pltpu.make_async_copy(total, out_i, sem.at[strips]))
    for copy in copies:
        copy.start()
    for copy in copies:
        copy.wait()


def solution(mesh):
    mems, tys, txs = mesh.shape["mem"], mesh.shape["ty"], mesh.shape["tx"]
    tiles = mems * tys

    def on_device(controls, perturbations, kx, ky, wet):
        rows, cols = kx.shape
        tile = rows // tiles
        levels = tiles // MEMBERS
        own = cols // LANES
        fold = rows // LANES
        sides = 2
        f32, bf16 = jnp.float32, jnp.bfloat16
        DMA, VMEM = pltpu.SemaphoreType.DMA, pltpu.VMEM
        deep = cols + 4 * GROUP
        folded = VMEM((fold, deep, LANES), f32)
        single = VMEM((deep, LANES), f32)
        final, total = pl.pallas_call(
            functools.partial(kernel, mems, tys, txs),
            out_shape=(VMEM((own, rows, LANES), f32), VMEM((levels, tile, cols), f32)),
            in_specs=[pl.BlockSpec(memory_space=pltpu.HBM)] * 5,
            out_specs=(pl.BlockSpec(memory_space=VMEM), pl.BlockSpec(memory_space=VMEM)),
            scratch_shapes=[
                VMEM((own, rows, LANES), bf16),
                VMEM((own, rows, LANES), bf16),
                VMEM((own, rows, LANES), jnp.int32),
                VMEM((own, rows, LANES), f32),
                VMEM((own, tiles, tile, LANES), bf16),
                VMEM((2, rows, LANES), f32),
                VMEM((2, fold, deep, LANES), f32),
                folded,
                folded,
                folded,
                folded,
                single,
                folded,
                single,
                single,
                VMEM((tiles, own, tile, LANES), jnp.int16),
                VMEM((tiles, own, tile, LANES), jnp.int16),
                VMEM((GROUP, LANES), f32),
                VMEM((tiles, GROUP, LANES), f32),
                DMA((5, own)),
                DMA((sides, 3)),
                DMA((sides, 3)),
                DMA((tiles,)),
                DMA((tiles,)),
                DMA((tiles,)),
                DMA((tiles,)),
            ],
            compiler_params=pltpu.CompilerParams(
                collective_id=0, has_side_effects=True, vmem_limit_bytes=62 * 2**20 + 2**19
            ),
        )(controls, perturbations, kx, ky, wet)
        return pl.pallas_call(
            store,
            out_shape=(
                jax.ShapeDtypeStruct((1, rows, cols), f32),
                jax.ShapeDtypeStruct((levels, tile, cols), f32),
            ),
            in_specs=[pl.BlockSpec(memory_space=VMEM)] * 2,
            out_specs=(pl.BlockSpec(memory_space=pltpu.HBM), pl.BlockSpec(memory_space=pltpu.HBM)),
            scratch_shapes=[DMA((own + 1,))],
            compiler_params=pltpu.CompilerParams(vmem_limit_bytes=8 * 2**20),
        )(final, total)

    in_specs = (
        P(("mem", "ty"), None, "tx"),
        P(None, ("mem", "ty"), "tx"),
        P(None, "tx"),
        P(None, "tx"),
        P(None, "tx"),
    )
    out_specs = (P(("mem", "ty"), None, "tx"), P(None, ("mem", "ty"), "tx"))
    return jax.shard_map(
        on_device, mesh=mesh, in_specs=in_specs, out_specs=out_specs, check_vma=False
    )
```

```python
import functools
import math

import jax
import jax.numpy as jnp
from jax import lax
from jax.experimental import pallas as pl
from jax.experimental.pallas import tpu as pltpu
from jax.sharding import PartitionSpec as P

MEMBERS = 8
STEPS = 8
LANES = 128
GROUP = 8
EDGE = 2 * GROUP
MASK = 64
PARTS = 2
CODE = 32767.0
MESH = pl.DeviceIdType.MESH


def kernel(
    mems, tys, txs, ctrl, pert, kx, ky, wet, final, out_i,
    kx_in, ky_in, wet_in, f_in, weights, plain, masked, ladder, fe, fn, south, zonal,
    send, recv, peak, peaks, partial, sums,
    in_sem, own_sem, edge_send, edge_recv, plane_send, plane_recv, peak_send, peak_recv,
    weight_send, weight_recv, sum_send, sum_recv, ack, go,
):
    tiles = mems * tys
    own, rows, _ = kx_in.shape
    cols = own * LANES
    fold = rows // LANES
    tile = rows // tiles
    levels = tiles // MEMBERS
    cells = ladder.at[0]
    me_mem, me_ty, me_tx = lax.axis_index("mem"), lax.axis_index("ty"), lax.axis_index("tx")
    chunk = tile * tys
    right, left = lax.rem(me_tx + 1, txs), lax.rem(me_tx + txs - 1, txs)
    sides = (right,) if txs == 2 else (right, left)

    def strip_loads(n, src, dst):
        return [
            pltpu.make_async_copy(src(pl.ds(c * LANES, LANES)), dst.at[c], in_sem.at[n, c]) for c in range(own)
        ]

    loads = [
        strip_loads(0, lambda s: kx.at[:, s], kx_in),
        strip_loads(1, lambda s: ky.at[:, s], ky_in),
        strip_loads(2, lambda s: wet.at[:, s], wet_in),
        strip_loads(3, lambda s: ctrl.at[0, :, s], f_in),
    ]
    order = (0, own - 1, *range(1, own - 1))
    for group in (loads[:3], loads[3:4]):
        for c in order:
            for load in group:
                load[c].start()

    barrier = pltpu.get_barrier_semaphore()
    odd = lax.rem(me_tx, 2) == 1

    def greet(semaphore, side):
        pl.semaphore_signal(semaphore, inc=1, device_id={"tx": side}, device_id_type=MESH)

    @pl.when(odd)
    def _():
        for side in sides:
            greet(barrier, side)

    @pl.when(jnp.logical_not(odd))
    def _():
        pl.semaphore_wait(barrier, len(sides))
        for side in sides:
            greet(ack, side)

    @pl.when(odd)
    def _():
        pl.semaphore_wait(ack, len(sides))

        for o in range(1, tys):
            pl.semaphore_signal(barrier, inc=1, device_id={"ty": lax.rem(me_ty + o, tys)}, device_id_type=MESH)
        for o in range(1, mems):
            pl.semaphore_signal(barrier, inc=1, device_id={"mem": lax.rem(me_mem + o, mems)}, device_id_type=MESH)

    def everyone_is_here():
        @pl.when(odd)
        def _():
            pl.semaphore_wait(barrier, mems + tys - 2)
            greet(go, left)

        @pl.when(jnp.logical_not(odd))
        def _():
            pl.semaphore_wait(go, 1)

    def turn_in(src, dst, c):
        for q in range(fold):
            dst[q, EDGE + c * LANES : EDGE + (c + 1) * LANES, :] = src[pl.ds(q, LANES, stride=fold), :].T

    def mask(c):
        for load in loads[:3]:
            load[c].wait()

        @pl.loop(0, rows // MASK)
        def _(n):
            at = pl.ds(pl.multiple_of(n * MASK, MASK), MASK)
            ocean = wet_in[c, at, :].astype(jnp.float32)
            plain[0, at, :] = kx_in[c, at, :].astype(jnp.float32) * ocean
            plain[1, at, :] = ky_in[c, at, :].astype(jnp.float32) * ocean

        for n in range(2):
            turn_in(plain.at[n], masked.at[n], c)

    def field(c):
        loads[3][c].wait()
        turn_in(f_in.at[c], cells, c)

    for c in order[:2]:
        mask(c)
    for c in order[:2]:
        field(c)

    edges = []
    for n, (side, src, dst) in enumerate(((left, EDGE, EDGE + cols), (right, EDGE + cols - GROUP, EDGE - GROUP))):
        for m, ref in enumerate((masked.at[0], masked.at[1], cells)):
            edges.append(
                pltpu.make_async_remote_copy(
                    src_ref=ref.at[:, pl.ds(src, GROUP), :], dst_ref=ref.at[:, pl.ds(dst, GROUP), :],
                    send_sem=edge_send.at[n, m], recv_sem=edge_recv.at[n, m],
                    device_id={"tx": side}, device_id_type=MESH,
                )
            )
            edges[-1].start()

    def weight_copy(o, m):
        to = lax.rem(me_ty + o, tys)
        return pltpu.make_async_remote_copy(
            src_ref=pert.at[m * tys + to], dst_ref=weights.at[me_ty, m],
            send_sem=weight_send.at[o, m], recv_sem=weight_recv.at[o, m],
            device_id={"ty": to}, device_id_type=MESH,
        )

    def own_weight(m):
        return pltpu.make_async_copy(pert.at[m * tys + me_ty], weights.at[me_ty, m], own_sem.at[m])

    everyone_is_here()
    for m in range(mems):
        for o in range(1, tys):
            weight_copy(o, m).start()
    for m in range(mems):
        own_weight(m).start()

    for c in order[2:]:
        mask(c)
    for c in order[2:]:
        field(c)

    def coefficients(base, count):
        at, after = pl.ds(base, count), pl.ds(base + 1, count)
        gys = [masked[1, q, at, :] for q in range(fold)]
        for q in range(fold):
            fe[q, at, :] = jnp.minimum(masked[0, q, at, :], masked[0, q, after, :])
            north = gys[q + 1] if q + 1 < fold else pltpu.roll(gys[0], LANES - 1, 1)
            fn[q, at, :] = jnp.minimum(gys[q], north)
        south[at, :] = jnp.minimum(gys[0], pltpu.roll(gys[-1], 1, 1))

    def largest(base, count, most):
        for q in range(fold):
            for g in range(0, count, GROUP):
                most = jnp.maximum(most, jnp.abs(cells[q, pl.ds(base + g, GROUP), :]))
        return most

    block = cols // 4
    for n in range(4):
        coefficients(EDGE + n * block, block if n < 3 else block - GROUP)

    most = lax.fori_loop(
        0, cols // GROUP // 8,
        lambda n, most: largest(pl.multiple_of(EDGE + n * 8 * GROUP, GROUP), 8 * GROUP, most),
        jnp.full((GROUP, LANES), 1e-30, jnp.float32),
    )

    for edge in edges:
        edge.wait()
    coefficients(EDGE - GROUP, GROUP)
    coefficients(EDGE + cols - GROUP, 2 * GROUP)
    most = largest(EDGE - GROUP, GROUP, largest(EDGE + cols, GROUP, most))
    most = jnp.max(jnp.max(most, axis=0, keepdims=True), axis=1, keepdims=True)
    peak[...] = jnp.broadcast_to(most, (GROUP, LANES))

    span = cols // PARTS
    share = own // PARTS
    reach = span + 2 * GROUP

    def advance(base, k):
        def at(g, shift=0):
            return pl.ds(base + g + shift, GROUP)

        def coefficient(g):
            return pl.ds(base - k + g, GROUP)

        groups = range(0, reach, GROUP)
        ups = [pltpu.roll(ladder[k - 1, 0, at(g, -1), :], LANES - 1, 1) for g in groups]
        downs = [pltpu.roll(ladder[k - 1, fold - 1, at(g, -1), :], 1, 1) for g in groups]
        for g in groups:
            here = [ladder[k - 1, q, at(g, -1), :] for q in range(fold)]
            flux_s = None
            for q in range(fold):
                flux_e = fe[q, coefficient(g), :] * (ladder[k - 1, q, at(g), :] - here[q])
                zonal[k - 1, q, at(g), :] = flux_e
                cell = here[q] + (flux_e - zonal[k - 1, q, at(g, -1), :])
                if q + 1 < fold:
                    flux_n = fn[q, coefficient(g), :] * (here[q + 1] - here[q])
                if q == 0:
                    cell = cell + flux_n
                elif q + 1 < fold:
                    cell = cell + (flux_n - flux_s)
                else:
                    cell = cell - flux_s
                ladder[k, q, at(g), :] = cell
                flux_s = flux_n
        for n, g in enumerate(groups):
            low, high = (ladder[k - 1, q, at(g, -1), :] for q in (0, fold - 1))
            ladder[k, 0, at(g), :] = ladder[k, 0, at(g), :] - south[coefficient(g), :] * (low - downs[n])
            ladder[k, fold - 1, at(g), :] = ladder[k, fold - 1, at(g), :] + fn[fold - 1, coefficient(g), :] * (ups[n] - high)

    def plane(o, src, dst, sems, at):
        return pltpu.make_async_remote_copy(
            src_ref=src, dst_ref=dst, send_sem=sems[0].at[at], recv_sem=sems[1].at[at],
            device_id={"mem": lax.rem(me_mem + o, mems)}, device_id_type=MESH,
        )

    def peak_copy(o):
        return plane(o, peak, peaks.at[o], (peak_send, peak_recv), o)

    def tile_copy(o, p):
        return plane(o, send.at[o, p], recv.at[o, p], (plane_send, plane_recv), (o, p))

    def sum_copy(o, p):
        to = lax.rem(me_ty + o, tys)
        return pltpu.make_async_remote_copy(
            src_ref=partial.at[to, p], dst_ref=sums.at[o, p],
            send_sem=sum_send.at[o, p], recv_sem=sum_recv.at[o, p],
            device_id={"ty": to}, device_id_type=MESH,
        )

    factor = CODE * lax.rsqrt(peak[:1, :1])

    @pl.loop(0, PARTS)
    def _(p):
        base = pl.multiple_of(EDGE - GROUP + p * span, GROUP)

        @pl.loop(1, STEPS + 1)
        def _(k):
            advance(base, k)

        for i in range(share):
            c = p * share + i
            at = pl.ds(pl.multiple_of(EDGE + STEPS + c * LANES, GROUP), LANES)
            for q in range(fold):
                final[c, pl.ds(q, LANES, stride=fold), :] = ladder[STEPS, q, at, :].T

        @pl.loop(1, mems)
        def _(o):
            to = lax.rem(me_mem + o, mems)
            for i in range(share):
                done = final[p * share + i, pl.ds(pl.multiple_of(to * chunk, chunk), chunk), :]
                code = done * lax.rsqrt(jnp.maximum(jnp.abs(done), 1e-37)) * factor
                code = jnp.round(jnp.clip(code, -CODE, CODE))
                send[o, p, i] = code.astype(jnp.int32).astype(jnp.int16)
            tile_copy(o, p).start()

            @pl.when(p == 0)
            def _():
                peak_copy(o).start()

    scale = 1.0 / math.sqrt(MEMBERS - 1)
    for o in range(1, mems):
        peak_copy(o).wait_recv()
    for m in range(mems):
        own_weight(m).wait()
        for o in range(1, tys):
            weight_copy(o, m).wait_recv()
    units = [peaks[o, :1, :1] * (scale / (CODE * CODE)) if o else None for o in range(mems)]

    for p in range(PARTS):
        for o in range(1, mems):
            tile_copy(o, p).wait_recv()

        @pl.loop(1, tys + 1)
        def _(step):
            z = lax.rem(me_ty + step, tys)
            for i in range(share):
                c = p * share + i
                lanes = slice(c * LANES, (c + 1) * LANES)
                at = pl.multiple_of(me_mem * chunk + z * tile, tile)
                total = weights[z, me_mem, :, lanes].astype(jnp.float32) * (final[c, pl.ds(at, tile), :] * scale)
                for o in range(1, mems):
                    m = lax.rem(me_mem - o + mems, mems)
                    code = recv[o, p, i, pl.ds(pl.multiple_of(z * tile, tile), tile), :].astype(jnp.float32)
                    total = total + weights[z, m, :, lanes].astype(jnp.float32) * (code * jnp.abs(code) * units[o])
                partial[z, p, i] = total

            @pl.when(step < tys)
            def _():
                sum_copy(step, p).start()

    for level in range(levels):
        out_i[level] = jnp.zeros(out_i.shape[1:], jnp.float32)
    for p in range(PARTS):
        for o in range(tys):
            if o:
                sum_copy(o, p).wait_recv()
            level = lax.rem(lax.rem(me_ty - o + tys, tys), levels)
            for i in range(share):
                c = p * share + i
                lanes = slice(c * LANES, (c + 1) * LANES)
                out_i[level, :, lanes] = out_i[level, :, lanes] + (sums[o, p, i] if o else partial[me_ty, p, i])

    for o in range(1, mems):
        peak_copy(o).wait_send()
        for p in range(PARTS):
            tile_copy(o, p).wait_send()
    for o in range(1, tys):
        for m in range(mems):
            weight_copy(o, m).wait_send()
        for p in range(PARTS):
            sum_copy(o, p).wait_send()


def store(final, total, out_s, out_i, sem):
    rows, strips = out_s.shape[1], out_s.shape[2] // LANES
    copies = [
        pltpu.make_async_copy(
            final.at[c], out_s.at[0, :, pl.ds(c * LANES, LANES)], sem.at[c]
        )
        for c in range(strips)
    ]
    copies.append(pltpu.make_async_copy(total, out_i, sem.at[strips]))
    for copy in copies:
        copy.start()
    for copy in copies:
        copy.wait()


def solution(mesh):
    mems, tys, txs = mesh.shape["mem"], mesh.shape["ty"], mesh.shape["tx"]
    tiles = mems * tys

    def on_device(controls, perturbations, kx, ky, wet):
        rows, cols = kx.shape
        tile = rows // tiles
        levels = tiles // MEMBERS
        own = cols // LANES
        fold = rows // LANES
        sides = 2
        f32, bf16 = jnp.float32, jnp.bfloat16
        DMA, VMEM = pltpu.SemaphoreType.DMA, pltpu.VMEM
        share = own // PARTS
        deep = cols + 3 * GROUP
        folded = VMEM((fold, deep, LANES), f32)
        single = VMEM((deep, LANES), f32)
        final, total = pl.pallas_call(
            functools.partial(kernel, mems, tys, txs),
            out_shape=(VMEM((own, rows, LANES), f32), VMEM((levels, tile, cols), f32)),
            in_specs=[pl.BlockSpec(memory_space=pltpu.HBM)] * 5,
            out_specs=(pl.BlockSpec(memory_space=VMEM), pl.BlockSpec(memory_space=VMEM)),
            scratch_shapes=[
                VMEM((own, rows, LANES), bf16),
                VMEM((own, rows, LANES), bf16),
                VMEM((own, rows, LANES), jnp.int32),
                VMEM((own, rows, LANES), f32),
                VMEM((tys, mems, tile, cols), bf16),
                VMEM((2, rows, LANES), f32),
                VMEM((2, fold, deep + GROUP, LANES), f32),
                VMEM((STEPS + 1, fold, deep, LANES), f32),
                folded,
                folded,
                single,
                VMEM((STEPS, fold, deep, LANES), f32),
                VMEM((mems, PARTS, share, tys * tile, LANES), jnp.int16),
                VMEM((mems, PARTS, share, tys * tile, LANES), jnp.int16),
                VMEM((GROUP, LANES), f32),
                VMEM((mems, GROUP, LANES), f32),
                VMEM((tys, PARTS, share, tile, LANES), f32),
                VMEM((tys, PARTS, share, tile, LANES), f32),
                DMA((4, own)),
                DMA((mems,)),
                DMA((sides, 3)),
                DMA((sides, 3)),
                DMA((mems, PARTS)),
                DMA((mems, PARTS)),
                DMA((mems,)),
                DMA((mems,)),
                DMA((tys, mems)),
                DMA((tys, mems)),
                DMA((tys, PARTS)),
                DMA((tys, PARTS)),
                pltpu.SemaphoreType.REGULAR,
                pltpu.SemaphoreType.REGULAR,
            ],
            compiler_params=pltpu.CompilerParams(
                collective_id=0, has_side_effects=True, vmem_limit_bytes=62 * 2**20 + 2**19
            ),
        )(controls, perturbations, kx, ky, wet)
        return pl.pallas_call(
            store,
            out_shape=(
                jax.ShapeDtypeStruct((1, rows, cols), f32),
                jax.ShapeDtypeStruct((levels, tile, cols), f32),
            ),
            in_specs=[pl.BlockSpec(memory_space=VMEM)] * 2,
            out_specs=(pl.BlockSpec(memory_space=pltpu.HBM), pl.BlockSpec(memory_space=pltpu.HBM)),
            scratch_shapes=[DMA((own + 1,))],
            compiler_params=pltpu.CompilerParams(vmem_limit_bytes=8 * 2**20),
        )(final, total)

    in_specs = (
        P(("mem", "ty"), None, "tx"),
        P(None, ("mem", "ty"), "tx"),
        P(None, "tx"),
        P(None, "tx"),
        P(None, "tx"),
    )
    out_specs = (P(("mem", "ty"), None, "tx"), P(None, ("mem", "ty"), "tx"))
    return jax.shard_map(
        on_device, mesh=mesh, in_specs=in_specs, out_specs=out_specs, check_vma=False
    )
```

```python
import functools
import math

import jax
import jax.numpy as jnp
from jax import lax
from jax.experimental import pallas as pl
from jax.experimental.pallas import tpu as pltpu
from jax.sharding import PartitionSpec as P

MEMBERS = 8
STEPS = 8
LANES = 128
GROUP = 8
EDGE = 3 * GROUP
MASK = 64
PARTS = 2
CODE = 32767.0
MESH = pl.DeviceIdType.MESH


def kernel(
    mems, tys, txs, ctrl, pert, kx, ky, wet, final, out_i,
    kx_in, ky_in, wet_in, f_in, weights, plain, masked, ladder, fe, fn, south,
    plane_out, plane_in, plane_unit, plane_units, sum_out, sum_in, sum_unit, sum_units, partial,
    in_sem, own_sem, edge_send, edge_recv, plane_send, plane_recv, sum_send, sum_recv,
    weight_send, weight_recv, ack, go,
):
    tiles = mems * tys
    own, rows, _ = kx_in.shape
    cols = own * LANES
    fold = rows // LANES
    tile = rows // tiles
    levels = tiles // MEMBERS
    cells = ladder.at[0]
    me_mem, me_ty, me_tx = lax.axis_index("mem"), lax.axis_index("ty"), lax.axis_index("tx")
    chunk = tile * tys
    right, left = lax.rem(me_tx + 1, txs), lax.rem(me_tx + txs - 1, txs)
    sides = (right,) if txs == 2 else (right, left)

    def strip_loads(n, src, dst):
        return [
            pltpu.make_async_copy(src(pl.ds(c * LANES, LANES)), dst.at[c], in_sem.at[n, c]) for c in range(own)
        ]

    loads = [
        strip_loads(0, lambda s: kx.at[:, s], kx_in),
        strip_loads(1, lambda s: ky.at[:, s], ky_in),
        strip_loads(2, lambda s: wet.at[:, s], wet_in),
        strip_loads(3, lambda s: ctrl.at[0, :, s], f_in),
    ]
    order = (0, own - 1, *range(1, own - 1))
    for group in (loads[:3], loads[3:4]):
        for c in order:
            for load in group:
                load[c].start()

    barrier = pltpu.get_barrier_semaphore()
    odd = lax.rem(me_tx, 2) == 1

    def greet(semaphore, side):
        pl.semaphore_signal(semaphore, inc=1, device_id={"tx": side}, device_id_type=MESH)

    @pl.when(odd)
    def _():
        for side in sides:
            greet(barrier, side)

    @pl.when(jnp.logical_not(odd))
    def _():
        pl.semaphore_wait(barrier, len(sides))
        for side in sides:
            greet(ack, side)

    @pl.when(odd)
    def _():
        pl.semaphore_wait(ack, len(sides))

        for o in range(1, tys):
            pl.semaphore_signal(barrier, inc=1, device_id={"ty": lax.rem(me_ty + o, tys)}, device_id_type=MESH)
        for o in range(1, mems):
            pl.semaphore_signal(barrier, inc=1, device_id={"mem": lax.rem(me_mem + o, mems)}, device_id_type=MESH)

    def everyone_is_here():
        @pl.when(odd)
        def _():
            pl.semaphore_wait(barrier, mems + tys - 2)
            greet(go, left)

        @pl.when(jnp.logical_not(odd))
        def _():
            pl.semaphore_wait(go, 1)

    def turn_in(src, dst, c):
        for q in range(fold):
            dst[q, EDGE + c * LANES : EDGE + (c + 1) * LANES, :] = src[pl.ds(q, LANES, stride=fold), :].T

    def mask(c):
        for load in loads[:3]:
            load[c].wait()

        @pl.loop(0, rows // MASK)
        def _(n):
            at = pl.ds(pl.multiple_of(n * MASK, MASK), MASK)
            ocean = wet_in[c, at, :].astype(jnp.float32)
            plain[0, at, :] = kx_in[c, at, :].astype(jnp.float32) * ocean
            plain[1, at, :] = ky_in[c, at, :].astype(jnp.float32) * ocean

        for n in range(2):
            turn_in(plain.at[n], masked.at[n], c)

    def field(c):
        loads[3][c].wait()
        turn_in(f_in.at[c], cells, c)

    for c in order[:2]:
        mask(c)
    for c in order[:2]:
        field(c)

    edges = []
    for n, (side, src, dst) in enumerate(((left, EDGE, EDGE + cols), (right, EDGE + cols - GROUP, EDGE - GROUP))):
        for m, ref in enumerate((masked.at[0], masked.at[1], cells)):
            edges.append(
                pltpu.make_async_remote_copy(
                    src_ref=ref.at[:, pl.ds(src, GROUP), :], dst_ref=ref.at[:, pl.ds(dst, GROUP), :],
                    send_sem=edge_send.at[n, m], recv_sem=edge_recv.at[n, m],
                    device_id={"tx": side}, device_id_type=MESH,
                )
            )
            edges[-1].start()

    def weight_copy(o, m):
        to = lax.rem(me_ty + o, tys)
        return pltpu.make_async_remote_copy(
            src_ref=pert.at[m * tys + to], dst_ref=weights.at[me_ty, m],
            send_sem=weight_send.at[o, m], recv_sem=weight_recv.at[o, m],
            device_id={"ty": to}, device_id_type=MESH,
        )

    def own_weight(m):
        return pltpu.make_async_copy(pert.at[m * tys + me_ty], weights.at[me_ty, m], own_sem.at[m])

    everyone_is_here()
    for m in range(mems):
        for o in range(1, tys):
            weight_copy(o, m).start()
    for m in range(mems):
        own_weight(m).start()

    for c in order[2:]:
        mask(c)
    for c in order[2:]:
        field(c)

    def coefficients(base, count):
        at, after = pl.ds(base, count), pl.ds(base + 1, count)
        gys = [masked[1, q, at, :] for q in range(fold)]
        for q in range(fold):
            fe[q, at, :] = jnp.minimum(masked[0, q, at, :], masked[0, q, after, :])
            north = gys[q + 1] if q + 1 < fold else pltpu.roll(gys[0], LANES - 1, 1)
            fn[q, at, :] = jnp.minimum(gys[q], north)
        south[at, :] = jnp.minimum(gys[0], pltpu.roll(gys[-1], 1, 1))

    block = cols // 4
    for n in range(4):
        coefficients(EDGE + n * block, block if n < 3 else block - GROUP)

    for edge in edges:
        edge.wait()
    coefficients(EDGE - GROUP, GROUP)
    coefficients(EDGE + cols - GROUP, 2 * GROUP)

    span = cols // PARTS
    share = own // PARTS
    reach = span + 2 * GROUP
    head = lax.broadcasted_iota(jnp.int32, (GROUP, LANES), 0) == 0

    def advance(base, k):
        def at(g, shift=0):
            return pl.ds(base + g + shift, GROUP)

        def coefficient(g):
            return pl.ds(base - k + g, GROUP)

        groups = range(0, reach, GROUP)
        ups = [pltpu.roll(ladder[k - 1, 0, at(g, -1), :], LANES - 1, 1) for g in groups]
        downs = [pltpu.roll(ladder[k - 1, fold - 1, at(g, -1), :], 1, 1) for g in groups]

        def flux_east(q, g, here):
            return fe[q, coefficient(g), :] * (ladder[k - 1, q, at(g), :] - here)

        before = [
            pltpu.roll(flux_east(q, -GROUP, ladder[k - 1, q, at(-GROUP, -1), :]), 1, 0) for q in range(fold)
        ]
        for n, g in enumerate(groups):
            here = [ladder[k - 1, q, at(g, -1), :] for q in range(fold)]
            flux_s = south[coefficient(g), :] * (here[0] - downs[n])
            for q in range(fold):
                north = here[q + 1] if q + 1 < fold else ups[n]
                flux_n = fn[q, coefficient(g), :] * (north - here[q])
                flux_e = flux_east(q, g, here[q])
                turned = pltpu.roll(flux_e, 1, 0)
                flux_w = jnp.where(head, before[q], turned)
                ladder[k, q, at(g), :] = here[q] + (flux_e - flux_w) + (flux_n - flux_s)
                before[q], flux_s = turned, flux_n

    def pair(kind, sems, at, to, sides):
        return [
            pltpu.make_async_remote_copy(
                src_ref=src, dst_ref=dst, send_sem=sems[0].at[n, *at], recv_sem=sems[1].at[n, *at],
                device_id={kind: to}, device_id_type=MESH,
            )
            for n, (src, dst) in enumerate(sides)
        ]

    def plane_copy(o, p):
        to = lax.rem(me_mem + o, mems)
        ends = ((plane_unit.at[o, p], plane_units.at[o, p]), (plane_out.at[o, p], plane_in.at[o, p]))
        return pair("mem", (plane_send, plane_recv), (o, p), to, ends)

    def sum_copy(o, p):
        to = lax.rem(me_ty + o, tys)
        ends = ((sum_unit.at[o, p], sum_units.at[o, p]), (sum_out.at[o, p], sum_in.at[o, p]))
        return pair("ty", (sum_send, sum_recv), (o, p), to, ends)

    def grouped(cells):
        return cells.reshape(cells.shape[0] // GROUP, GROUP, LANES)

    def encode(cells, unit, code):
        cells = [grouped(cell) for cell in cells]
        most = functools.reduce(jnp.maximum, [jnp.max(jnp.abs(cell), axis=0) for cell in cells])
        most = jnp.maximum(most, 1e-30)
        unit[...] = most * (1.0 / (CODE * CODE))
        factor = (CODE * lax.rsqrt(most))[None]
        for n, cell in enumerate(cells):
            root = cell * lax.rsqrt(jnp.maximum(jnp.abs(cell), 1e-37)) * factor
            root = jnp.round(jnp.clip(root, -CODE, CODE)).astype(jnp.int32)
            code[n] = root.reshape(code.shape[1:]).astype(jnp.int16)

    def decode(code, unit):
        code = grouped(code.astype(jnp.float32))
        return (code * jnp.abs(code) * unit[None]).reshape(-1, LANES)

    @pl.loop(0, PARTS)
    def _(p):
        base = pl.multiple_of(EDGE - GROUP + p * span, GROUP)

        @pl.loop(1, STEPS + 1)
        def _(k):
            advance(base, k)

        for i in range(share):
            c = p * share + i
            at = pl.ds(pl.multiple_of(EDGE + STEPS + c * LANES, GROUP), LANES)
            for q in range(fold):
                final[c, pl.ds(q, LANES, stride=fold), :] = ladder[STEPS, q, at, :].T

        @pl.loop(1, mems)
        def _(o):
            at = pl.ds(pl.multiple_of(lax.rem(me_mem + o, mems) * chunk, chunk), chunk)
            encode([final[p * share + i, at, :] for i in range(share)], plane_unit.at[o, p], plane_out.at[o, p])
            for copy in plane_copy(o, p):
                copy.start()

    scale = 1.0 / math.sqrt(MEMBERS - 1)
    for m in range(mems):
        own_weight(m).wait()
        for o in range(1, tys):
            weight_copy(o, m).wait_recv()
    lanes = [slice(c * LANES, (c + 1) * LANES) for c in range(own)]

    for p in range(PARTS):
        for o in range(1, mems):
            for copy in plane_copy(o, p):
                copy.wait_recv()

        def total(z, i):
            c = p * share + i
            at = pl.multiple_of(me_mem * chunk + z * tile, tile)
            cells = weights[z, me_mem, :, lanes[c]].astype(jnp.float32) * (final[c, pl.ds(at, tile), :] * scale)
            for o in range(1, mems):
                m = lax.rem(me_mem - o + mems, mems)
                got = decode(plane_in[o, p, i, pl.ds(pl.multiple_of(z * tile, tile), tile), :], plane_units[o, p] * scale)
                cells = cells + weights[z, m, :, lanes[c]].astype(jnp.float32) * got
            return cells

        @pl.loop(1, tys)
        def _(o):
            z = lax.rem(me_ty + o, tys)
            encode([total(z, i) for i in range(share)], sum_unit.at[o, p], sum_out.at[o, p])
            for copy in sum_copy(o, p):
                copy.start()

        for i in range(share):
            partial[p * share + i] = total(me_ty, i)

    for level in range(levels):
        out_i[level] = jnp.zeros(out_i.shape[1:], jnp.float32)
    for p in range(PARTS):
        for o in range(tys):
            if o:
                for copy in sum_copy(o, p):
                    copy.wait_recv()
            level = lax.rem(lax.rem(me_ty - o + tys, tys), levels)
            for i in range(share):
                c = p * share + i
                got = decode(sum_in[o, p, i], sum_units[o, p]) if o else partial[c]
                out_i[level, :, lanes[c]] = out_i[level, :, lanes[c]] + got

    for p in range(PARTS):
        for o in range(1, mems):
            for copy in plane_copy(o, p):
                copy.wait_send()
        for o in range(1, tys):
            for copy in sum_copy(o, p):
                copy.wait_send()
    for o in range(1, tys):
        for m in range(mems):
            weight_copy(o, m).wait_send()


def store(final, total, out_s, out_i, sem):
    rows, strips = out_s.shape[1], out_s.shape[2] // LANES
    copies = [
        pltpu.make_async_copy(
            final.at[c], out_s.at[0, :, pl.ds(c * LANES, LANES)], sem.at[c]
        )
        for c in range(strips)
    ]
    copies.append(pltpu.make_async_copy(total, out_i, sem.at[strips]))
    for copy in copies:
        copy.start()
    for copy in copies:
        copy.wait()


def solution(mesh):
    mems, tys, txs = mesh.shape["mem"], mesh.shape["ty"], mesh.shape["tx"]
    tiles = mems * tys

    def on_device(controls, perturbations, kx, ky, wet):
        rows, cols = kx.shape
        tile = rows // tiles
        levels = tiles // MEMBERS
        own = cols // LANES
        fold = rows // LANES
        sides = 2
        f32, bf16 = jnp.float32, jnp.bfloat16
        DMA, VMEM = pltpu.SemaphoreType.DMA, pltpu.VMEM
        share = own // PARTS
        deep = cols + 4 * GROUP
        folded = VMEM((fold, deep, LANES), f32)
        single = VMEM((deep, LANES), f32)
        final, total = pl.pallas_call(
            functools.partial(kernel, mems, tys, txs),
            out_shape=(VMEM((own, rows, LANES), f32), VMEM((levels, tile, cols), f32)),
            in_specs=[pl.BlockSpec(memory_space=pltpu.HBM)] * 5,
            out_specs=(pl.BlockSpec(memory_space=VMEM), pl.BlockSpec(memory_space=VMEM)),
            scratch_shapes=[
                VMEM((own, rows, LANES), bf16),
                VMEM((own, rows, LANES), bf16),
                VMEM((own, rows, LANES), jnp.int32),
                VMEM((own, rows, LANES), f32),
                VMEM((tys, mems, tile, cols), bf16),
                VMEM((2, rows, LANES), f32),
                VMEM((2, fold, deep + GROUP, LANES), f32),
                VMEM((STEPS + 1, fold, deep, LANES), f32),
                folded,
                folded,
                single,
                VMEM((mems, PARTS, share, tys * tile, LANES), jnp.int16),
                VMEM((mems, PARTS, share, tys * tile, LANES), jnp.int16),
                VMEM((mems, PARTS, GROUP, LANES), f32),
                VMEM((mems, PARTS, GROUP, LANES), f32),
                VMEM((tys, PARTS, share, tile, LANES), jnp.int16),
                VMEM((tys, PARTS, share, tile, LANES), jnp.int16),
                VMEM((tys, PARTS, GROUP, LANES), f32),
                VMEM((tys, PARTS, GROUP, LANES), f32),
                VMEM((own, tile, LANES), f32),
                DMA((4, own)),
                DMA((mems,)),
                DMA((sides, 3)),
                DMA((sides, 3)),
                DMA((2, mems, PARTS)),
                DMA((2, mems, PARTS)),
                DMA((2, tys, PARTS)),
                DMA((2, tys, PARTS)),
                DMA((tys, mems)),
                DMA((tys, mems)),
                pltpu.SemaphoreType.REGULAR,
                pltpu.SemaphoreType.REGULAR,
            ],
            compiler_params=pltpu.CompilerParams(
                collective_id=0, has_side_effects=True, vmem_limit_bytes=62 * 2**20 + 2**19
            ),
        )(controls, perturbations, kx, ky, wet)
        return pl.pallas_call(
            store,
            out_shape=(
                jax.ShapeDtypeStruct((1, rows, cols), f32),
                jax.ShapeDtypeStruct((levels, tile, cols), f32),
            ),
            in_specs=[pl.BlockSpec(memory_space=VMEM)] * 2,
            out_specs=(pl.BlockSpec(memory_space=pltpu.HBM), pl.BlockSpec(memory_space=pltpu.HBM)),
            scratch_shapes=[DMA((own + 1,))],
            compiler_params=pltpu.CompilerParams(vmem_limit_bytes=8 * 2**20),
        )(final, total)

    in_specs = (
        P(("mem", "ty"), None, "tx"),
        P(None, ("mem", "ty"), "tx"),
        P(None, "tx"),
        P(None, "tx"),
        P(None, "tx"),
    )
    out_specs = (P(("mem", "ty"), None, "tx"), P(None, ("mem", "ty"), "tx"))
    return jax.shard_map(
        on_device, mesh=mesh, in_specs=in_specs, out_specs=out_specs, check_vma=False
    )
```

```python
import functools
import math

import jax
import jax.numpy as jnp
from jax import lax
from jax.experimental import pallas as pl
from jax.experimental.pallas import tpu as pltpu
from jax.sharding import PartitionSpec as P

MEMBERS = 8
STEPS = 8
LANES = 128
GROUP = 8
EDGE = 3 * GROUP
MASK = 64
PARTS = 2
CODE = 32767.0
MESH = pl.DeviceIdType.MESH


def kernel(
    mems, tys, txs, ctrl, pert, kx, ky, wet, final, out_i,
    kx_in, ky_in, wet_in, f_in, weights, plain, masked, ladder, fe, fn, south,
    plane_out, plane_in, plane_unit, plane_units, sum_out, sum_in, sum_unit, sum_units, partial,
    in_sem, own_sem, edge_send, edge_recv, plane_send, plane_recv, sum_send, sum_recv,
    weight_send, weight_recv, ack, go,
):
    tiles = mems * tys
    own, rows, _ = kx_in.shape
    cols = own * LANES
    fold = rows // LANES
    tile = rows // tiles
    levels = tiles // MEMBERS
    cells = ladder.at[0]
    me_mem, me_ty, me_tx = lax.axis_index("mem"), lax.axis_index("ty"), lax.axis_index("tx")
    chunk = tile * tys
    right, left = lax.rem(me_tx + 1, txs), lax.rem(me_tx + txs - 1, txs)
    sides = (right,) if txs == 2 else (right, left)

    def strip_loads(n, src, dst):
        return [
            pltpu.make_async_copy(src(pl.ds(c * LANES, LANES)), dst.at[c], in_sem.at[n, c]) for c in range(own)
        ]

    loads = [
        strip_loads(0, lambda s: kx.at[:, s], kx_in),
        strip_loads(1, lambda s: ky.at[:, s], ky_in),
        strip_loads(2, lambda s: wet.at[:, s], wet_in),
        strip_loads(3, lambda s: ctrl.at[0, :, s], f_in),
    ]
    order = (0, own - 1, *range(1, own - 1))
    for group in (loads[:3], loads[3:4]):
        for c in order:
            for load in group:
                load[c].start()

    barrier = pltpu.get_barrier_semaphore()
    odd = lax.rem(me_tx, 2) == 1

    def greet(semaphore, side):
        pl.semaphore_signal(semaphore, inc=1, device_id={"tx": side}, device_id_type=MESH)

    @pl.when(odd)
    def _():
        for side in sides:
            greet(barrier, side)

    @pl.when(jnp.logical_not(odd))
    def _():
        pl.semaphore_wait(barrier, len(sides))
        for side in sides:
            greet(ack, side)

    @pl.when(odd)
    def _():
        pl.semaphore_wait(ack, len(sides))

        for o in range(1, tys):
            pl.semaphore_signal(barrier, inc=1, device_id={"ty": lax.rem(me_ty + o, tys)}, device_id_type=MESH)
        for o in range(1, mems):
            pl.semaphore_signal(barrier, inc=1, device_id={"mem": lax.rem(me_mem + o, mems)}, device_id_type=MESH)

    def everyone_is_here():
        @pl.when(odd)
        def _():
            pl.semaphore_wait(barrier, mems + tys - 2)
            greet(go, left)

        @pl.when(jnp.logical_not(odd))
        def _():
            pl.semaphore_wait(go, 1)

    def turn_in(src, dst, c):
        for q in range(fold):
            dst[q, EDGE + c * LANES : EDGE + (c + 1) * LANES, :] = src[pl.ds(q, LANES, stride=fold), :].T

    def mask(c):
        for load in loads[:3]:
            load[c].wait()

        @pl.loop(0, rows // MASK)
        def _(n):
            at = pl.ds(pl.multiple_of(n * MASK, MASK), MASK)
            ocean = wet_in[c, at, :].astype(jnp.float32)
            plain[0, at, :] = kx_in[c, at, :].astype(jnp.float32) * ocean
            plain[1, at, :] = ky_in[c, at, :].astype(jnp.float32) * ocean

        for n in range(2):
            turn_in(plain.at[n], masked.at[n], c)

    def field(c):
        loads[3][c].wait()
        turn_in(f_in.at[c], cells, c)

    for c in order[:2]:
        mask(c)
    for c in order[:2]:
        field(c)

    edges = []
    for n, (side, src, dst) in enumerate(((left, EDGE, EDGE + cols), (right, EDGE + cols - GROUP, EDGE - GROUP))):
        for m, ref in enumerate((masked.at[0], masked.at[1], cells)):
            edges.append(
                pltpu.make_async_remote_copy(
                    src_ref=ref.at[:, pl.ds(src, GROUP), :], dst_ref=ref.at[:, pl.ds(dst, GROUP), :],
                    send_sem=edge_send.at[n, m], recv_sem=edge_recv.at[n, m],
                    device_id={"tx": side}, device_id_type=MESH,
                )
            )
            edges[-1].start()

    def weight_copy(o):
        to = lax.rem(me_ty + o, tys)
        return pltpu.make_async_remote_copy(
            src_ref=pert.at[:, to], dst_ref=weights.at[me_ty],
            send_sem=weight_send.at[o], recv_sem=weight_recv.at[o],
            device_id={"ty": to}, device_id_type=MESH,
        )

    own_weight = pltpu.make_async_copy(pert.at[:, me_ty], weights.at[me_ty], own_sem)
    everyone_is_here()
    for o in range(1, tys):
        weight_copy(o).start()
    own_weight.start()

    for c in order[2:]:
        mask(c)
    for c in order[2:]:
        field(c)

    def coefficients(base, count):
        at, after = pl.ds(base, count), pl.ds(base + 1, count)
        gys = [masked[1, q, at, :] for q in range(fold)]
        for q in range(fold):
            fe[q, at, :] = jnp.minimum(masked[0, q, at, :], masked[0, q, after, :])
            north = gys[q + 1] if q + 1 < fold else pltpu.roll(gys[0], LANES - 1, 1)
            fn[q, at, :] = jnp.minimum(gys[q], north)
        south[at, :] = jnp.minimum(gys[0], pltpu.roll(gys[-1], 1, 1))

    block = cols // 4
    for n in range(4):
        coefficients(EDGE + n * block, block if n < 3 else block - GROUP)

    for edge in edges:
        edge.wait()
    coefficients(EDGE - GROUP, GROUP)
    coefficients(EDGE + cols - GROUP, 2 * GROUP)

    span = cols // PARTS
    share = own // PARTS
    reach = span + 3 * GROUP
    head = lax.broadcasted_iota(jnp.int32, (GROUP, LANES), 0) == 0

    def advance(base, k):
        def at(g, shift=0):
            return pl.ds(base + g + shift, GROUP)

        groups = range(0, reach, GROUP)
        ups = [pltpu.roll(ladder[k - 1, 0, at(g), :], LANES - 1, 1) for g in groups]
        downs = [pltpu.roll(ladder[k - 1, fold - 1, at(g), :], 1, 1) for g in groups]

        def flux_east(q, g, here):
            return fe[q, at(g), :] * (ladder[k - 1, q, at(g, 1), :] - here)

        before = [
            pltpu.roll(flux_east(q, -GROUP, ladder[k - 1, q, at(-GROUP), :]), 1, 0) for q in range(fold)
        ]
        for n, g in enumerate(groups):
            here = [ladder[k - 1, q, at(g), :] for q in range(fold)]
            flux_s = south[at(g), :] * (here[0] - downs[n])
            for q in range(fold):
                north = here[q + 1] if q + 1 < fold else ups[n]
                flux_n = fn[q, at(g), :] * (north - here[q])
                flux_e = flux_east(q, g, here[q])
                turned = pltpu.roll(flux_e, 1, 0)
                flux_w = jnp.where(head, before[q], turned)
                ladder[k, q, at(g), :] = here[q] + (flux_e - flux_w) + (flux_n - flux_s)
                before[q], flux_s = turned, flux_n

    def pair(kind, sems, at, to, sides):
        return [
            pltpu.make_async_remote_copy(
                src_ref=src, dst_ref=dst, send_sem=sems[0].at[n, *at], recv_sem=sems[1].at[n, *at],
                device_id={kind: to}, device_id_type=MESH,
            )
            for n, (src, dst) in enumerate(sides)
        ]

    def plane_copy(o, p):
        to = lax.rem(me_mem + o, mems)
        ends = ((plane_unit.at[o, p], plane_units.at[o, p]), (plane_out.at[o, p], plane_in.at[o, p]))
        return pair("mem", (plane_send, plane_recv), (o, p), to, ends)

    def sum_copy(o, p):
        to = lax.rem(me_ty + o, tys)
        ends = ((sum_unit.at[o, p], sum_units.at[o, p]), (sum_out.at[o, p], sum_in.at[o, p]))
        return pair("ty", (sum_send, sum_recv), (o, p), to, ends)

    def grouped(cells):
        return cells.reshape(cells.shape[0] // GROUP, GROUP, LANES)

    def encode(cells, unit, code):
        cells = [grouped(cell) for cell in cells]
        most = functools.reduce(jnp.maximum, [jnp.max(jnp.abs(cell), axis=0) for cell in cells])
        most = jnp.maximum(most, 1e-30)
        unit[...] = most * (1.0 / (CODE * CODE))
        factor = (CODE * lax.rsqrt(most))[None]
        for n, cell in enumerate(cells):
            root = cell * lax.rsqrt(jnp.maximum(jnp.abs(cell), 1e-37)) * factor
            root = jnp.round(jnp.clip(root, -CODE, CODE)).astype(jnp.int32)
            code[n] = root.reshape(code.shape[1:]).astype(jnp.int16)

    def decode(code, unit):
        code = grouped(code.astype(jnp.float32))
        return (code * jnp.abs(code) * unit[None]).reshape(-1, LANES)

    @pl.loop(0, PARTS)
    def _(p):
        base = pl.multiple_of(EDGE - GROUP + p * (span - GROUP), GROUP)

        @pl.loop(1, STEPS + 1)
        def _(k):
            advance(base, k)

        for i in range(share):
            c = p * share + i
            at = pl.ds(pl.multiple_of(EDGE + c * LANES, GROUP), LANES)
            for q in range(fold):
                final[c, pl.ds(q, LANES, stride=fold), :] = ladder[STEPS, q, at, :].T

        @pl.loop(1, mems)
        def _(o):
            at = pl.ds(pl.multiple_of(lax.rem(me_mem + o, mems) * chunk, chunk), chunk)
            encode([final[p * share + i, at, :] for i in range(share)], plane_unit.at[o, p], plane_out.at[o, p])
            for copy in plane_copy(o, p):
                copy.start()

    scale = 1.0 / math.sqrt(MEMBERS - 1)
    own_weight.wait()
    for o in range(1, tys):
        weight_copy(o).wait_recv()
    lanes = [slice(c * LANES, (c + 1) * LANES) for c in range(own)]

    for p in range(PARTS):
        for o in range(1, mems):
            for copy in plane_copy(o, p):
                copy.wait_recv()

        def total(z, i):
            c = p * share + i
            at = pl.multiple_of(me_mem * chunk + z * tile, tile)
            cells = weights[z, me_mem, :, lanes[c]].astype(jnp.float32) * (final[c, pl.ds(at, tile), :] * scale)
            for o in range(1, mems):
                m = lax.rem(me_mem - o + mems, mems)
                got = decode(plane_in[o, p, i, pl.ds(pl.multiple_of(z * tile, tile), tile), :], plane_units[o, p] * scale)
                cells = cells + weights[z, m, :, lanes[c]].astype(jnp.float32) * got
            return cells

        @pl.loop(1, tys)
        def _(o):
            z = lax.rem(me_ty + o, tys)
            encode([total(z, i) for i in range(share)], sum_unit.at[o, p], sum_out.at[o, p])
            for copy in sum_copy(o, p):
                copy.start()

        for i in range(share):
            partial[p * share + i] = total(me_ty, i)

    for level in range(levels):
        out_i[level] = jnp.zeros(out_i.shape[1:], jnp.float32)
    for p in range(PARTS):
        for o in range(tys):
            if o:
                for copy in sum_copy(o, p):
                    copy.wait_recv()
            level = lax.rem(lax.rem(me_ty - o + tys, tys), levels)
            for i in range(share):
                c = p * share + i
                got = decode(sum_in[o, p, i], sum_units[o, p]) if o else partial[c]
                out_i[level, :, lanes[c]] = out_i[level, :, lanes[c]] + got

    for p in range(PARTS):
        for o in range(1, mems):
            for copy in plane_copy(o, p):
                copy.wait_send()
        for o in range(1, tys):
            for copy in sum_copy(o, p):
                copy.wait_send()
    for o in range(1, tys):
        weight_copy(o).wait_send()


def store(final, total, out_s, out_i, sem):
    rows, strips = out_s.shape[1], out_s.shape[2] // LANES
    copies = [
        pltpu.make_async_copy(
            final.at[c], out_s.at[0, :, pl.ds(c * LANES, LANES)], sem.at[c]
        )
        for c in range(strips)
    ]
    copies.append(pltpu.make_async_copy(total, out_i, sem.at[strips]))
    for copy in copies:
        copy.start()
    for copy in copies:
        copy.wait()


def solution(mesh):
    mems, tys, txs = mesh.shape["mem"], mesh.shape["ty"], mesh.shape["tx"]
    tiles = mems * tys

    def on_device(controls, perturbations, kx, ky, wet):
        rows, cols = kx.shape
        tile = rows // tiles
        levels = tiles // MEMBERS
        own = cols // LANES
        fold = rows // LANES
        sides = 2
        f32, bf16 = jnp.float32, jnp.bfloat16
        DMA, VMEM = pltpu.SemaphoreType.DMA, pltpu.VMEM
        share = own // PARTS
        deep = cols + 5 * GROUP
        folded = VMEM((fold, deep, LANES), f32)
        single = VMEM((deep, LANES), f32)
        final, total = pl.pallas_call(
            functools.partial(kernel, mems, tys, txs),
            out_shape=(VMEM((own, rows, LANES), f32), VMEM((levels, tile, cols), f32)),
            in_specs=[pl.BlockSpec(memory_space=pltpu.HBM)] * 5,
            out_specs=(pl.BlockSpec(memory_space=VMEM), pl.BlockSpec(memory_space=VMEM)),
            scratch_shapes=[
                VMEM((own, rows, LANES), bf16),
                VMEM((own, rows, LANES), bf16),
                VMEM((own, rows, LANES), jnp.int32),
                VMEM((own, rows, LANES), f32),
                VMEM((tys, mems, tile, cols), bf16),
                VMEM((2, rows, LANES), f32),
                VMEM((2, fold, deep + GROUP, LANES), f32),
                VMEM((STEPS + 1, fold, deep, LANES), f32),
                folded,
                folded,
                single,
                VMEM((mems, PARTS, share, tys * tile, LANES), jnp.int16),
                VMEM((mems, PARTS, share, tys * tile, LANES), jnp.int16),
                VMEM((mems, PARTS, GROUP, LANES), f32),
                VMEM((mems, PARTS, GROUP, LANES), f32),
                VMEM((tys, PARTS, share, tile, LANES), jnp.int16),
                VMEM((tys, PARTS, share, tile, LANES), jnp.int16),
                VMEM((tys, PARTS, GROUP, LANES), f32),
                VMEM((tys, PARTS, GROUP, LANES), f32),
                VMEM((own, tile, LANES), f32),
                DMA((4, own)),
                DMA,
                DMA((sides, 3)),
                DMA((sides, 3)),
                DMA((2, mems, PARTS)),
                DMA((2, mems, PARTS)),
                DMA((2, tys, PARTS)),
                DMA((2, tys, PARTS)),
                DMA((tys,)),
                DMA((tys,)),
                pltpu.SemaphoreType.REGULAR,
                pltpu.SemaphoreType.REGULAR,
            ],
            compiler_params=pltpu.CompilerParams(
                collective_id=0, has_side_effects=True, vmem_limit_bytes=62 * 2**20 + 2**19
            ),
        )(controls, perturbations.reshape(mems, tys, tile, cols), kx, ky, wet)
        return pl.pallas_call(
            store,
            out_shape=(
                jax.ShapeDtypeStruct((1, rows, cols), f32),
                jax.ShapeDtypeStruct((levels, tile, cols), f32),
            ),
            in_specs=[pl.BlockSpec(memory_space=VMEM)] * 2,
            out_specs=(pl.BlockSpec(memory_space=pltpu.HBM), pl.BlockSpec(memory_space=pltpu.HBM)),
            scratch_shapes=[DMA((own + 1,))],
            compiler_params=pltpu.CompilerParams(vmem_limit_bytes=8 * 2**20),
        )(final, total)

    in_specs = (
        P(("mem", "ty"), None, "tx"),
        P(None, ("mem", "ty"), "tx"),
        P(None, "tx"),
        P(None, "tx"),
        P(None, "tx"),
    )
    out_specs = (P(("mem", "ty"), None, "tx"), P(None, ("mem", "ty"), "tx"))
    return jax.shard_map(
        on_device, mesh=mesh, in_specs=in_specs, out_specs=out_specs, check_vma=False
    )
```

```python
import functools
import math

import jax
import jax.numpy as jnp
from jax import lax
from jax.experimental import pallas as pl
from jax.experimental.pallas import tpu as pltpu
from jax.sharding import PartitionSpec as P

MEMBERS = 8
STEPS = 8
LANES = 128
GROUP = 8
EDGE = 3 * GROUP
MASK = 64
PARTS = 1
CODE = 32767.0
MESH = pl.DeviceIdType.MESH


def kernel(
    mems, tys, txs, ctrl, pert, kx, ky, wet, final, out_i,
    kx_in, ky_in, wet_in, f_in, weights, plain, masked, ladder, fe, fn, south,
    plane_out, plane_in, plane_unit, plane_units, sum_out, sum_in, sum_unit, sum_units, partial,
    in_sem, own_sem, edge_send, edge_recv, plane_send, plane_recv, sum_send, sum_recv,
    weight_send, weight_recv, ack, go,
):
    tiles = mems * tys
    own, rows, _ = kx_in.shape
    cols = own * LANES
    fold = rows // LANES
    tile = rows // tiles
    levels = tiles // MEMBERS
    cells = ladder.at[0]
    me_mem, me_ty, me_tx = lax.axis_index("mem"), lax.axis_index("ty"), lax.axis_index("tx")
    chunk = tile * tys
    right, left = lax.rem(me_tx + 1, txs), lax.rem(me_tx + txs - 1, txs)
    sides = (right,) if txs == 2 else (right, left)

    def strip_loads(n, src, dst):
        return [
            pltpu.make_async_copy(src(pl.ds(c * LANES, LANES)), dst.at[c], in_sem.at[n, c]) for c in range(own)
        ]

    loads = [
        strip_loads(0, lambda s: kx.at[:, s], kx_in),
        strip_loads(1, lambda s: ky.at[:, s], ky_in),
        strip_loads(2, lambda s: wet.at[:, s], wet_in),
        strip_loads(3, lambda s: ctrl.at[0, :, s], f_in),
    ]
    order = (0, own - 1, *range(1, own - 1))
    for group in (loads[:3], loads[3:4]):
        for c in order:
            for load in group:
                load[c].start()

    barrier = pltpu.get_barrier_semaphore()
    odd = lax.rem(me_tx, 2) == 1

    def greet(semaphore, side):
        pl.semaphore_signal(semaphore, inc=1, device_id={"tx": side}, device_id_type=MESH)

    @pl.when(odd)
    def _():
        for side in sides:
            greet(barrier, side)

    @pl.when(jnp.logical_not(odd))
    def _():
        pl.semaphore_wait(barrier, len(sides))
        for side in sides:
            greet(ack, side)

    @pl.when(odd)
    def _():
        pl.semaphore_wait(ack, len(sides))

        for o in range(1, tys):
            pl.semaphore_signal(barrier, inc=1, device_id={"ty": lax.rem(me_ty + o, tys)}, device_id_type=MESH)
        for o in range(1, mems):
            pl.semaphore_signal(barrier, inc=1, device_id={"mem": lax.rem(me_mem + o, mems)}, device_id_type=MESH)

    def everyone_is_here():
        @pl.when(odd)
        def _():
            pl.semaphore_wait(barrier, mems + tys - 2)
            greet(go, left)

        @pl.when(jnp.logical_not(odd))
        def _():
            pl.semaphore_wait(go, 1)

    def turn_in(src, dst, c):
        for q in range(fold):
            dst[q, EDGE + c * LANES : EDGE + (c + 1) * LANES, :] = src[pl.ds(q, LANES, stride=fold), :].T

    def mask(c):
        for load in loads[:3]:
            load[c].wait()

        @pl.loop(0, rows // MASK)
        def _(n):
            at = pl.ds(pl.multiple_of(n * MASK, MASK), MASK)
            ocean = wet_in[c, at, :].astype(jnp.float32)
            plain[0, at, :] = kx_in[c, at, :].astype(jnp.float32) * ocean
            plain[1, at, :] = ky_in[c, at, :].astype(jnp.float32) * ocean

        for n in range(2):
            turn_in(plain.at[n], masked.at[n], c)

    def field(c):
        loads[3][c].wait()
        turn_in(f_in.at[c], cells, c)

    for c in order[:2]:
        mask(c)
    for c in order[:2]:
        field(c)

    edges = []
    for n, (side, src, dst) in enumerate(((left, EDGE, EDGE + cols), (right, EDGE + cols - GROUP, EDGE - GROUP))):
        for m, ref in enumerate((masked.at[0], masked.at[1], cells)):
            edges.append(
                pltpu.make_async_remote_copy(
                    src_ref=ref.at[:, pl.ds(src, GROUP), :], dst_ref=ref.at[:, pl.ds(dst, GROUP), :],
                    send_sem=edge_send.at[n, m], recv_sem=edge_recv.at[n, m],
                    device_id={"tx": side}, device_id_type=MESH,
                )
            )
            edges[-1].start()

    def weight_copy(o):
        to = lax.rem(me_ty + o, tys)
        return pltpu.make_async_remote_copy(
            src_ref=pert.at[:, to], dst_ref=weights.at[me_ty],
            send_sem=weight_send.at[o], recv_sem=weight_recv.at[o],
            device_id={"ty": to}, device_id_type=MESH,
        )

    own_weight = pltpu.make_async_copy(pert.at[:, me_ty], weights.at[me_ty], own_sem)
    everyone_is_here()
    for o in range(1, tys):
        weight_copy(o).start()
    own_weight.start()

    for c in order[2:]:
        mask(c)
    for c in order[2:]:
        field(c)

    def coefficients(base, count):
        at, after = pl.ds(base, count), pl.ds(base + 1, count)
        gys = [masked[1, q, at, :] for q in range(fold)]
        for q in range(fold):
            fe[q, at, :] = jnp.minimum(masked[0, q, at, :], masked[0, q, after, :])
            north = gys[q + 1] if q + 1 < fold else pltpu.roll(gys[0], LANES - 1, 1)
            fn[q, at, :] = jnp.minimum(gys[q], north)
        south[at, :] = jnp.minimum(gys[0], pltpu.roll(gys[-1], 1, 1))

    block = cols // 4
    for n in range(4):
        coefficients(EDGE + n * block, block if n < 3 else block - GROUP)

    for edge in edges:
        edge.wait()
    coefficients(EDGE - GROUP, GROUP)
    coefficients(EDGE + cols - GROUP, 2 * GROUP)

    span = cols // PARTS
    share = own // PARTS
    reach = span + 3 * GROUP
    head = lax.broadcasted_iota(jnp.int32, (GROUP, LANES), 0) == 0

    def advance(base, k):
        def at(g, shift=0):
            return pl.ds(base + g + shift, GROUP)

        groups = range(0, reach, GROUP)
        ups = [pltpu.roll(ladder[k - 1, 0, at(g), :], LANES - 1, 1) for g in groups]
        downs = [pltpu.roll(ladder[k - 1, fold - 1, at(g), :], 1, 1) for g in groups]

        def flux_east(q, g, here):
            return fe[q, at(g), :] * (ladder[k - 1, q, at(g, 1), :] - here)

        before = [
            pltpu.roll(flux_east(q, -GROUP, ladder[k - 1, q, at(-GROUP), :]), 1, 0) for q in range(fold)
        ]
        for n, g in enumerate(groups):
            here = [ladder[k - 1, q, at(g), :] for q in range(fold)]
            flux_s = south[at(g), :] * (here[0] - downs[n])
            for q in range(fold):
                north = here[q + 1] if q + 1 < fold else ups[n]
                flux_n = fn[q, at(g), :] * (north - here[q])
                flux_e = flux_east(q, g, here[q])
                turned = pltpu.roll(flux_e, 1, 0)
                flux_w = jnp.where(head, before[q], turned)
                ladder[k, q, at(g), :] = here[q] + (flux_e - flux_w) + (flux_n - flux_s)
                before[q], flux_s = turned, flux_n

    def pair(kind, sems, at, to, sides):
        return [
            pltpu.make_async_remote_copy(
                src_ref=src, dst_ref=dst, send_sem=sems[0].at[n, *at], recv_sem=sems[1].at[n, *at],
                device_id={kind: to}, device_id_type=MESH,
            )
            for n, (src, dst) in enumerate(sides)
        ]

    def plane_copy(o, p):
        to = lax.rem(me_mem + o, mems)
        ends = ((plane_unit.at[o, p], plane_units.at[o, p]), (plane_out.at[o, p], plane_in.at[o, p]))
        return pair("mem", (plane_send, plane_recv), (o, p), to, ends)

    def sum_copy(o, p):
        to = lax.rem(me_ty + o, tys)
        ends = ((sum_unit.at[o, p], sum_units.at[o, p]), (sum_out.at[o, p], sum_in.at[o, p]))
        return pair("ty", (sum_send, sum_recv), (o, p), to, ends)

    def grouped(cells):
        return cells.reshape(cells.shape[0] // GROUP, GROUP, LANES)

    def encode(cells, unit, code):
        cells = [grouped(cell) for cell in cells]
        most = functools.reduce(jnp.maximum, [jnp.max(jnp.abs(cell), axis=0) for cell in cells])
        most = jnp.maximum(most, 1e-30)
        unit[...] = most * (1.0 / (CODE * CODE))
        factor = (CODE * lax.rsqrt(most))[None]
        for n, cell in enumerate(cells):
            root = cell * lax.rsqrt(jnp.maximum(jnp.abs(cell), 1e-37)) * factor
            root = jnp.round(jnp.clip(root, -CODE, CODE)).astype(jnp.int32)
            code[n] = root.reshape(code.shape[1:]).astype(jnp.int16)

    def decode(code, unit):
        code = grouped(code.astype(jnp.float32))
        return (code * jnp.abs(code) * unit[None]).reshape(-1, LANES)

    @pl.loop(0, PARTS)
    def _(p):
        base = pl.multiple_of(EDGE - GROUP + p * (span - GROUP), GROUP)

        @pl.loop(1, STEPS + 1)
        def _(k):
            advance(base, k)

        for i in range(share):
            c = p * share + i
            at = pl.ds(pl.multiple_of(EDGE + c * LANES, GROUP), LANES)
            for q in range(fold):
                final[c, pl.ds(q, LANES, stride=fold), :] = ladder[STEPS, q, at, :].T

        @pl.loop(1, mems)
        def _(o):
            at = pl.ds(pl.multiple_of(lax.rem(me_mem + o, mems) * chunk, chunk), chunk)
            encode([final[p * share + i, at, :] for i in range(share)], plane_unit.at[o, p], plane_out.at[o, p])
            for copy in plane_copy(o, p):
                copy.start()

    scale = 1.0 / math.sqrt(MEMBERS - 1)
    own_weight.wait()
    for o in range(1, tys):
        weight_copy(o).wait_recv()
    lanes = [slice(c * LANES, (c + 1) * LANES) for c in range(own)]

    for p in range(PARTS):
        for o in range(1, mems):
            for copy in plane_copy(o, p):
                copy.wait_recv()

        def total(z, i):
            c = p * share + i
            at = pl.multiple_of(me_mem * chunk + z * tile, tile)
            cells = weights[z, me_mem, :, lanes[c]].astype(jnp.float32) * (final[c, pl.ds(at, tile), :] * scale)
            for o in range(1, mems):
                m = lax.rem(me_mem - o + mems, mems)
                got = decode(plane_in[o, p, i, pl.ds(pl.multiple_of(z * tile, tile), tile), :], plane_units[o, p] * scale)
                cells = cells + weights[z, m, :, lanes[c]].astype(jnp.float32) * got
            return cells

        @pl.loop(1, tys)
        def _(o):
            z = lax.rem(me_ty + o, tys)
            encode([total(z, i) for i in range(share)], sum_unit.at[o, p], sum_out.at[o, p])
            for copy in sum_copy(o, p):
                copy.start()

        for i in range(share):
            partial[p * share + i] = total(me_ty, i)

    for level in range(levels):
        out_i[level] = jnp.zeros(out_i.shape[1:], jnp.float32)
    for p in range(PARTS):
        for o in range(tys):
            if o:
                for copy in sum_copy(o, p):
                    copy.wait_recv()
            level = lax.rem(lax.rem(me_ty - o + tys, tys), levels)
            for i in range(share):
                c = p * share + i
                got = decode(sum_in[o, p, i], sum_units[o, p]) if o else partial[c]
                out_i[level, :, lanes[c]] = out_i[level, :, lanes[c]] + got

    for p in range(PARTS):
        for o in range(1, mems):
            for copy in plane_copy(o, p):
                copy.wait_send()
        for o in range(1, tys):
            for copy in sum_copy(o, p):
                copy.wait_send()
    for o in range(1, tys):
        weight_copy(o).wait_send()


def store(final, total, out_s, out_i, sem):
    rows, strips = out_s.shape[1], out_s.shape[2] // LANES
    copies = [
        pltpu.make_async_copy(
            final.at[c], out_s.at[0, :, pl.ds(c * LANES, LANES)], sem.at[c]
        )
        for c in range(strips)
    ]
    copies.append(pltpu.make_async_copy(total, out_i, sem.at[strips]))
    for copy in copies:
        copy.start()
    for copy in copies:
        copy.wait()


def solution(mesh):
    mems, tys, txs = mesh.shape["mem"], mesh.shape["ty"], mesh.shape["tx"]
    tiles = mems * tys

    def on_device(controls, perturbations, kx, ky, wet):
        rows, cols = kx.shape
        tile = rows // tiles
        levels = tiles // MEMBERS
        own = cols // LANES
        fold = rows // LANES
        sides = 2
        f32, bf16 = jnp.float32, jnp.bfloat16
        DMA, VMEM = pltpu.SemaphoreType.DMA, pltpu.VMEM
        share = own // PARTS
        deep = cols + 7 * GROUP
        folded = VMEM((fold, deep, LANES), f32)
        single = VMEM((deep, LANES), f32)
        final, total = pl.pallas_call(
            functools.partial(kernel, mems, tys, txs),
            out_shape=(VMEM((own, rows, LANES), f32), VMEM((levels, tile, cols), f32)),
            in_specs=[pl.BlockSpec(memory_space=pltpu.HBM)] * 5,
            out_specs=(pl.BlockSpec(memory_space=VMEM), pl.BlockSpec(memory_space=VMEM)),
            scratch_shapes=[
                VMEM((own, rows, LANES), bf16),
                VMEM((own, rows, LANES), bf16),
                VMEM((own, rows, LANES), jnp.int32),
                VMEM((own, rows, LANES), f32),
                VMEM((tys, mems, tile, cols), bf16),
                VMEM((2, rows, LANES), f32),
                VMEM((2, fold, deep + GROUP, LANES), f32),
                VMEM((STEPS + 1, fold, deep, LANES), f32),
                folded,
                folded,
                single,
                VMEM((mems, PARTS, share, tys * tile, LANES), jnp.int16),
                VMEM((mems, PARTS, share, tys * tile, LANES), jnp.int16),
                VMEM((mems, PARTS, GROUP, LANES), f32),
                VMEM((mems, PARTS, GROUP, LANES), f32),
                VMEM((tys, PARTS, share, tile, LANES), jnp.int16),
                VMEM((tys, PARTS, share, tile, LANES), jnp.int16),
                VMEM((tys, PARTS, GROUP, LANES), f32),
                VMEM((tys, PARTS, GROUP, LANES), f32),
                VMEM((own, tile, LANES), f32),
                DMA((4, own)),
                DMA,
                DMA((sides, 3)),
                DMA((sides, 3)),
                DMA((2, mems, PARTS)),
                DMA((2, mems, PARTS)),
                DMA((2, tys, PARTS)),
                DMA((2, tys, PARTS)),
                DMA((tys,)),
                DMA((tys,)),
                pltpu.SemaphoreType.REGULAR,
                pltpu.SemaphoreType.REGULAR,
            ],
            compiler_params=pltpu.CompilerParams(
                collective_id=0, has_side_effects=True, vmem_limit_bytes=62 * 2**20 + 2**19
            ),
        )(controls, perturbations.reshape(mems, tys, tile, cols), kx, ky, wet)
        return pl.pallas_call(
            store,
            out_shape=(
                jax.ShapeDtypeStruct((1, rows, cols), f32),
                jax.ShapeDtypeStruct((levels, tile, cols), f32),
            ),
            in_specs=[pl.BlockSpec(memory_space=VMEM)] * 2,
            out_specs=(pl.BlockSpec(memory_space=pltpu.HBM), pl.BlockSpec(memory_space=pltpu.HBM)),
            scratch_shapes=[DMA((own + 1,))],
            compiler_params=pltpu.CompilerParams(vmem_limit_bytes=8 * 2**20),
        )(final, total)

    in_specs = (
        P(("mem", "ty"), None, "tx"),
        P(None, ("mem", "ty"), "tx"),
        P(None, "tx"),
        P(None, "tx"),
        P(None, "tx"),
    )
    out_specs = (P(("mem", "ty"), None, "tx"), P(None, ("mem", "ty"), "tx"))
    return jax.shard_map(
        on_device, mesh=mesh, in_specs=in_specs, out_specs=out_specs, check_vma=False
    )
```
